768 devices in a mesh: pts: 192 (over z, x_lo, y), ctr: 4 (over x_hi, core).
Axes of the slice: x: 4 (x_hi: 2, x_lo: 2; x = x_hi * 2 + x_lo), y: 8, z: 12, core: 2. Of those that a mesh axis runs over, the one named last changes fastest.
Arguments:
- points: bfloat16 [32, 393216], P(None, 'pts'), may hold values from -6 to 6
- centres: bfloat16 [32, 32768], P(None, 'ctr'), may hold values from -6 to 6
- coef: float32 [16, 32768], P(None, 'ctr'), may hold values from -6 to 6
- resid: float32 [16, 32768], P(None, 'ctr'), may hold values from -6 to 6
- direction: float32 [16, 32768], P(None, 'ctr'), may hold values from -6 to 6
- precond: float32 [32768], P('ctr'), may hold values from 0.5 to 4
Outputs:
- coef_next: float32 [16, 32768], P(None, 'ctr')
- resid_next: float32 [16, 32768], P(None, 'ctr')
- dir_next: float32 [16, 32768], P(None, 'ctr')
The draws below stay inside these ranges and needn't reach their ends.
All inputs are finite; a program needn't handle non-finite values.
Results may differ from the reference program's by a relative error of at most 0.0012.
Values may be sent and summed in bfloat16 or wider, within the bound.
A program may use at most 128 MiB of HBM per device.

```python
import math
import jax
import jax.numpy as jnp
from jax import lax

FEAT = 32
CTR_DEV = 8192
P_DEV = 2048
TARGETS = 16
CENTRES = 32768
NPTS = 393216
N_PTS = 192
N_CTR = 4


def block_scale(rng, shape, shards, low, high):
    def one(axis_at, shards_of):
        steps = jax.random.uniform(jax.random.fold_in(jax.random.fold_in(rng, 6), axis_at), (shards_of,), jnp.float32, low / len(shards), high / len(shards))
        return jnp.repeat(jnp.exp(steps), shape[axis_at] // shards_of).reshape((-1,) + (1,) * (len(shape) - axis_at - 1))

    gain = one(*shards[0])
    for cut in shards[1:]:
        gain = gain * one(*cut)
    return gain


def centred(key, dims, width, most, cuts=(), held_as=jnp.bfloat16):
    values = width * jax.random.normal(key, dims, jnp.float32)
    if cuts:
        values = values * block_scale(key, dims, cuts, -0.22, 0.18)
    return jnp.clip(values, -most, most).astype(held_as)


def setup_inputs(seed: int = 0) -> dict:
    seeds = jax.random.split(jax.random.key(seed), 7)
    points = centred(seeds[0], (FEAT, NPTS), 1.0, 6.0, ((1, 192),))
    centres = centred(seeds[1], (FEAT, CENTRES), 1.0, 6.0, ((1, 4),))
    coef = centred(seeds[2], (TARGETS, CENTRES), 1.0, 6.0, ((1, 4),), jnp.float32)
    resid = centred(seeds[3], (TARGETS, CENTRES), 1.0, 6.0, ((1, 4),), jnp.float32)
    direction = centred(seeds[4], (TARGETS, CENTRES), 1.0, 6.0, ((1, 4),), jnp.float32)
    precond = jnp.clip(jnp.exp(math.log(4.0) - 2.0794415 * jax.random.uniform(seeds[5], (CENTRES,), jnp.float32) ** block_scale(seeds[5], (CENTRES,), ((0, 4),), -0.2, 0.2)), 0.5, 4.0)
    return dict(points=points, centres=centres, coef=coef, resid=resid, direction=direction, precond=precond)


def reference(points, centres, coef, resid, direction, precond):
    cent32 = centres.astype(jnp.float32)
    csq = jnp.sum(cent32 * cent32, axis=0)
    dirb = direction.astype(jnp.bfloat16)
    blocks = points.reshape(FEAT, N_PTS, P_DEV).transpose(1, 0, 2)

    def step(acc, block):
        pts32 = block.astype(jnp.float32)
        xsq = jnp.sum(pts32 * pts32, axis=0)
        cross = lax.dot_general(block, centres, (((0,), (0,)), ((), ())), preferred_element_type=jnp.float32)
        kern = jnp.exp(-0.125 * (xsq[:, None] + csq[None, :] - 2.0 * cross)).astype(jnp.bfloat16)
        fitted = jnp.zeros((TARGETS, P_DEV), jnp.float32)
        for group in range(N_CTR):
            low = group * CTR_DEV
            part = lax.dot_general(dirb[:, low:low + CTR_DEV], kern[:, low:low + CTR_DEV], (((1,), (1,)), ((), ())), preferred_element_type=jnp.float32)
            part = lax.optimization_barrier(part.astype(jnp.bfloat16))
            fitted = fitted + part.astype(jnp.float32)
        acc = acc + jnp.dot(fitted.astype(jnp.bfloat16), kern, preferred_element_type=jnp.float32)
        return acc, None

    colsum, _ = lax.scan(step, jnp.zeros((TARGETS, CENTRES), jnp.float32), blocks)
    rz = jnp.sum(resid * resid * precond[None, :], axis=1)
    image = colsum * (2048.0 / NPTS) + 0.5 * direction
    alpha = rz / jnp.sum(direction * image, axis=1)
    coef_next = coef + alpha[:, None] * direction
    resid_next = resid - alpha[:, None] * image
    scaled = precond[None, :] * resid_next
    rz_new = jnp.sum(resid_next * scaled, axis=1)
    dir_next = scaled + (rz_new / rz)[:, None] * direction
    return coef_next, resid_next, dir_next
```

```python
import functools
import math

import jax
import jax.numpy as jnp
from jax import lax
from jax.experimental import pallas as pl
from jax.experimental.pallas import tpu as pltpu
from jax.sharding import PartitionSpec as P

MESH = pl.DeviceIdType.MESH
F32 = jnp.float32
BF16 = jnp.bfloat16
LOG2E = math.log2(math.e)

GROUPS = 4
PLANE = 16
DEPTH = 12
STRIDE = 3
PCH = 4
MCH = 4
LANES = 128


def three_terms(v):
    hi = v.astype(BF16)
    rest = v - hi.astype(F32)
    mid = rest.astype(BF16)
    lo = (rest - mid.astype(F32)).astype(BF16)
    return hi, mid, lo


def tail_rows(width, first, second):
    row = lax.broadcasted_iota(jnp.int32, (32, width), 0)
    out = jnp.zeros((32, width), F32)
    for k, v in enumerate((*first, *second)):
        out = jnp.where(row == k, v if isinstance(v, float) else v.astype(F32), out)
    return out.astype(BF16)


def kernel(
    pts_ref, cen_ref, dir_ref, res_ref, prec_ref, q_ref, scal_ref,
    xa, ca, dirb, kern, fits, col, rsb, z1b, z2b, agb, scb,
    fit_s, fit_r, rs_s, rs_r, z1_s, z1_r, z2_s, z2_r, ag_s, ag_r, sc_s, sc_r,
):
    npts = pts_ref.shape[1]
    ctrs = cen_ref.shape[1]
    tgt = dir_ref.shape[0]
    pch = npts // PCH
    mch = ctrs // MCH
    pts = lax.axis_index("pts")
    ctr = lax.axis_index("ctr")
    z = pts // PLANE
    mine = pts % PLANE
    third, step = z // STRIDE, z % STRIDE

    def ctr_peer(d):
        return {"ctr": (ctr + d) % GROUPS}

    def plane_peer(d):
        return {"pts": z * PLANE + (mine + d) % PLANE}

    def z_peer(d):
        return {"pts": (z + d) % DEPTH * PLANE + mine}

    barrier = pltpu.get_barrier_semaphore()
    peers = [ctr_peer(d) for d in range(1, GROUPS)]
    peers += [plane_peer(d) for d in range(1, PLANE)]
    peers += [z_peer(d) for d in (3, 6, 9, 1, 11)]
    for peer in peers:
        pl.semaphore_signal(barrier, inc=1, device_id=peer, device_id_type=MESH)

    def send(src, dst, s, r, peer):
        return pltpu.make_async_remote_copy(
            src_ref=src, dst_ref=dst, send_sem=s, recv_sem=r, device_id=peer, device_id_type=MESH
        )

    x32 = pts_ref[...].astype(F32)
    hi, mid, lo = three_terms(x32 * (0.25 * LOG2E))
    xa[0:32, :] = hi
    xa[32:64, :] = mid
    xa[64:96, :] = lo
    xsq = jnp.sum(x32 * x32, axis=0, keepdims=True) * (-0.125 * LOG2E)
    xa[96:128, :] = tail_rows(npts, (1.0, 1.0, 1.0), three_terms(xsq))

    def centre_block(k, carry):
        m0 = pl.multiple_of(k * 1024, 1024)
        c = cen_ref[:, pl.ds(m0, 1024)]
        c32 = c.astype(F32)
        csq = jnp.sum(c32 * c32, axis=0, keepdims=True) * (-0.125 * LOG2E)
        tail = tail_rows(1024, three_terms(csq), (1.0, 1.0, 1.0))
        ca[pl.ds(m0, 1024), :] = jnp.concatenate([c, c, c, tail], axis=0).T
        dirb[:, pl.ds(m0, 1024)] = dir_ref[:, pl.ds(m0, 1024)].astype(BF16)
        return carry

    lax.fori_loop(0, ctrs // 1024, centre_block, 0)

    def fit_copy(i, d):
        return send(
            fits.at[ctr, i], fits.at[ctr, i], fit_s.at[i, d], fit_r.at[i, d], ctr_peer(d)
        )

    def point_chunk(i):
        n0 = pl.multiple_of(i * pch, pch)

        def block(j, acc):
            m0 = pl.multiple_of(j * 2048, 2048)
            s = jnp.dot(
                ca[pl.ds(m0, 2048), :], xa[:, pl.ds(n0, pch)], preferred_element_type=F32
            )
            k = jnp.exp2(s).astype(BF16)
            kern[pl.ds(m0, 2048), pl.ds(n0, pch)] = k
            return acc + jnp.dot(dirb[:, pl.ds(m0, 2048)], k, preferred_element_type=F32)

        acc = lax.fori_loop(0, ctrs // 2048, block, jnp.zeros((tgt, pch), F32))
        fits[ctr, i] = acc.astype(BF16)

    def first_chunk(i, carry):
        point_chunk(i)
        for d in range(1, GROUPS):
            fit_copy(i, d).start()
        return carry

    point_chunk(0)
    pl.semaphore_wait(barrier, len(peers))
    for d in range(1, GROUPS):
        fit_copy(0, d).start()
    lax.fori_loop(1, PCH, first_chunk, 0)

    fitted = []
    for i in range(PCH):
        for d in range(1, GROUPS):
            fit_copy(i, d).wait()
        total = fits[0, i].astype(F32)
        for g in range(1, GROUPS):
            total = total + fits[g, i].astype(F32)
        fitted.append(total.astype(BF16))
    fitb = jnp.concatenate(fitted, axis=1)

    def rs_copy(c, d):
        return send(
            col.at[c, (mine + d) % PLANE], rsb.at[c, mine], rs_s.at[c, d], rs_r.at[c, d], plane_peer(d)
        )

    def ag_copy(c, d):
        return send(
            agb.at[c, mine], agb.at[c, mine], ag_s.at[c, d], ag_r.at[c, d], plane_peer(d)
        )

    def z1_copy(c, d):
        return send(
            z1b.at[c, third], z1b.at[c, third], z1_s.at[c, d], z1_r.at[c, d], z_peer(d * STRIDE)
        )

    def z2_copy(c, d):
        return send(
            z2b.at[c, step], z2b.at[c, step], z2_s.at[c, d], z2_r.at[c, d], z_peer((1, DEPTH - 1)[d])
        )

    def columns(c, carry):
        for h in range(mch // 512):
            m0 = pl.multiple_of(c * mch + h * 512, 512)
            part = lax.dot_general(
                fitb, kern[pl.ds(m0, 512), :], (((1,), (1,)), ((), ())), preferred_element_type=F32
            )
            for j in range(4):
                col[c, 4 * h + j] = part[:, j * LANES : (j + 1) * LANES]
        rsb[c, mine] = col[c, mine]
        for d in range(1, PLANE):
            rs_copy(c, d).start()
        return carry

    lax.fori_loop(0, MCH, columns, 0)

    def summed(ref, c, count):
        total = ref[c, 0]
        for k in range(1, count):
            total = total + ref[c, k]
        return total

    def to_z1(c, carry):
        for d in range(1, PLANE):
            rs_copy(c, d).wait()
        z1b[c, third] = summed(rsb, c, PLANE)
        for d in range(1, DEPTH // STRIDE):
            z1_copy(c, d).start()
        return carry

    def to_z2(c, carry):
        for d in range(1, DEPTH // STRIDE):
            z1_copy(c, d).wait()
        z2b[c, step] = summed(z1b, c, DEPTH // STRIDE)
        for d in range(2):
            z2_copy(c, d).start()
        return carry

    def to_ag(c, carry):
        for d in range(2):
            z2_copy(c, d).wait()
        agb[c, mine] = summed(z2b, c, STRIDE)
        for d in range(1, PLANE):
            ag_copy(c, d).start()
        return carry

    lax.fori_loop(0, MCH, to_z1, 0)
    lax.fori_loop(0, MCH, to_z2, 0)
    lax.fori_loop(0, MCH, to_ag, 0)

    scale = 2048.0 / (npts * DEPTH * PLANE)

    def finish(c, sums):
        for d in range(1, PLANE):
            ag_copy(c, d).wait()
        rr, rq, qq, dq = sums
        for k in range(PLANE):
            at = pl.ds(pl.multiple_of(c * mch + k * LANES, LANES), LANES)
            dirv, resv, prec = dir_ref[:, at], res_ref[:, at], prec_ref[:, at]
            image = agb[c, k] * scale + 0.5 * dirv
            q_ref[:, at] = image
            pr = prec * resv
            rr = rr + pr * resv
            rq = rq + pr * image
            qq = qq + prec * image * image
            dq = dq + dirv * image
        return rr, rq, qq, dq

    zero = jnp.zeros((tgt, LANES), F32)
    sums = lax.fori_loop(0, MCH, finish, (zero, zero, zero, zero))
    for k, v in enumerate(sums):
        scb[ctr, k] = v

    def sc_copy(d):
        return send(scb.at[ctr], scb.at[ctr], sc_s.at[d], sc_r.at[d], ctr_peer(d))

    for d in range(1, GROUPS):
        sc_copy(d).start()
    for d in range(1, GROUPS):
        sc_copy(d).wait()
    rr, rq, qq, dq = [
        jnp.sum(scb[0, k] + scb[1, k] + scb[2, k] + scb[3, k], axis=1, keepdims=True)
        for k in range(4)
    ]
    alpha = rr / dq
    rz_new = rr - 2.0 * alpha * rq + alpha * alpha * qq
    scal_ref[0] = jnp.broadcast_to(alpha, (tgt, LANES))
    scal_ref[1] = jnp.broadcast_to(rz_new / rr, (tgt, LANES))


def shards(points, centres, coef, resid, direction, precond):
    tgt, ctrs = direction.shape
    feat, npts = points.shape
    prec = precond[None, :]
    vm = pl.BlockSpec(memory_space=pltpu.VMEM)
    dma = pltpu.SemaphoreType.DMA
    share = (tgt, LANES)
    image, scal = pl.pallas_call(
        kernel,
        out_shape=(
            jax.ShapeDtypeStruct((tgt, ctrs), F32),
            jax.ShapeDtypeStruct((2, tgt, LANES), F32),
        ),
        in_specs=[vm] * 5,
        out_specs=(vm, vm),
        scratch_shapes=[
            pltpu.VMEM((128, npts), BF16),
            pltpu.VMEM((ctrs, 128), BF16),
            pltpu.VMEM((tgt, ctrs), BF16),
            pltpu.VMEM((ctrs, npts), BF16),
            pltpu.VMEM((GROUPS, PCH, tgt, npts // PCH), BF16),
            pltpu.VMEM((MCH, PLANE, *share), F32),
            pltpu.VMEM((MCH, PLANE, *share), F32),
            pltpu.VMEM((MCH, DEPTH // STRIDE, *share), F32),
            pltpu.VMEM((MCH, STRIDE, *share), F32),
            pltpu.VMEM((MCH, PLANE, *share), F32),
            pltpu.VMEM((GROUPS, 4, *share), F32),
            dma((PCH, GROUPS)), dma((PCH, GROUPS)),
            dma((MCH, PLANE)), dma((MCH, PLANE)),
            dma((MCH, DEPTH // STRIDE)), dma((MCH, DEPTH // STRIDE)),
            dma((MCH, 2)), dma((MCH, 2)),
            dma((MCH, PLANE)), dma((MCH, PLANE)),
            dma((GROUPS,)), dma((GROUPS,)),
        ],
        compiler_params=pltpu.CompilerParams(
            collective_id=0, has_side_effects=True, vmem_limit_bytes=60 << 20
        ),
        name="cg_step",
    )(points, centres, direction, resid, prec)
    alpha = scal[0, :, :1]
    beta = scal[1, :, :1]
    resid_new = resid - alpha * image
    return coef + alpha * direction, resid_new, prec * resid_new + beta * direction


def solution(mesh):
    return jax.shard_map(
        shards,
        mesh=mesh,
        in_specs=(P(None, "pts"), *[P(None, "ctr")] * 4, P("ctr")),
        out_specs=(P(None, "ctr"),) * 3,
        check_vma=False,
    )
```

```python
import functools
import math

import jax
import jax.numpy as jnp
from jax import lax
from jax.experimental import pallas as pl
from jax.experimental.pallas import tpu as pltpu
from jax.sharding import PartitionSpec as P

MESH = pl.DeviceIdType.MESH
F32 = jnp.float32
BF16 = jnp.bfloat16
LOG2E = math.log2(math.e)

GROUPS = 4
PLANE = 16
DEPTH = 12
PCH = 4
MCH = 4
EARLY = 2
LANES = 128


def three_terms(v):
    hi = v.astype(BF16)
    rest = v - hi.astype(F32)
    mid = rest.astype(BF16)
    lo = (rest - mid.astype(F32)).astype(BF16)
    return hi, mid, lo


def tail_rows(width, first, second):
    row = lax.broadcasted_iota(jnp.int32, (32, width), 0)
    out = jnp.zeros((32, width), F32)
    for k, v in enumerate((*first, *second)):
        out = jnp.where(row == k, v if isinstance(v, float) else v.astype(F32), out)
    return out.astype(BF16)


def kernel(
    pts_hbm, cen_hbm, dir_hbm, res_hbm, prec_hbm, q_ref, scal_ref,
    pts_ref, cen_ref, dir_ref, res_ref, prec_ref,
    xa, ca, dirb, kern0, kern1, kern2, kern3, fits, early, col, rsb, zb, agb, scb,
    in_s, fit_s, fit_r, rs_s, rs_r, z_s, z_r, ag_s, ag_r, sc_s, sc_r,
):
    npts = pts_ref.shape[1]
    tgt, ctrs = dir_ref.shape
    pch = npts // PCH
    mch = ctrs // MCH
    kerns = (kern0, kern1, kern2, kern3)
    pts = lax.axis_index("pts")
    ctr = lax.axis_index("ctr")
    z = pts // PLANE
    mine = pts % PLANE

    loads = [
        pltpu.make_async_copy(src, dst, in_s.at[k])
        for k, (src, dst) in enumerate(
            [(pts_hbm, pts_ref), (cen_hbm, cen_ref), (dir_hbm, dir_ref), (res_hbm, res_ref), (prec_hbm, prec_ref)]
        )
    ]
    for load in loads:
        load.start()

    def ctr_peer(d):
        return {"ctr": (ctr + d) % GROUPS}

    def plane_peer(d):
        return {"pts": z * PLANE + (mine + d) % PLANE}

    def z_peer(d):
        return {"pts": (z + d) % DEPTH * PLANE + mine}

    barrier = pltpu.get_barrier_semaphore()
    peers = [ctr_peer(d) for d in range(1, GROUPS)]
    peers += [plane_peer(d) for d in range(1, PLANE)]
    peers += [z_peer(d) for d in range(1, DEPTH)]
    for peer in peers:
        pl.semaphore_signal(barrier, inc=1, device_id=peer, device_id_type=MESH)

    def send(src, dst, s, r, peer):
        return pltpu.make_async_remote_copy(
            src_ref=src, dst_ref=dst, send_sem=s, recv_sem=r, device_id=peer, device_id_type=MESH
        )

    loads[0].wait()
    x32 = pts_ref[...].astype(F32)
    hi, mid, lo = three_terms(x32 * (0.25 * LOG2E))
    xa[0:32, :] = hi
    xa[32:64, :] = mid
    xa[64:96, :] = lo
    xsq = jnp.sum(x32 * x32, axis=0, keepdims=True) * (-0.125 * LOG2E)
    xa[96:128, :] = tail_rows(npts, (1.0, 1.0, 1.0), three_terms(xsq))
    loads[1].wait()
    loads[2].wait()

    def centre_block(k, carry):
        m0 = pl.multiple_of(k * 1024, 1024)
        c = cen_ref[:, pl.ds(m0, 1024)]
        c32 = c.astype(F32)
        csq = jnp.sum(c32 * c32, axis=0, keepdims=True) * (-0.125 * LOG2E)
        tail = tail_rows(1024, three_terms(csq), (1.0, 1.0, 1.0))
        ca[pl.ds(m0, 1024), :] = jnp.concatenate([c, c, c, tail], axis=0).T
        dirb[:, pl.ds(m0, 1024)] = dir_ref[:, pl.ds(m0, 1024)].astype(BF16)
        return carry

    lax.fori_loop(0, ctrs // 1024, centre_block, 0)

    def fit_copy(i, d):
        return send(
            fits.at[ctr, i], fits.at[ctr, i], fit_s.at[i, d], fit_r.at[i, d], ctr_peer(d)
        )

    for i in range(PCH + 1):

        def block(j, acc, i=i):
            m0 = pl.multiple_of(j * 2048, 2048)
            if i < PCH:
                s = jnp.dot(
                    ca[pl.ds(m0, 2048), :], xa[:, i * pch : (i + 1) * pch], preferred_element_type=F32
                )
                kerns[i][pl.ds(m0, 2048), :] = jnp.exp2(s).astype(BF16)
            if i > 0:
                acc = acc + jnp.dot(
                    dirb[:, pl.ds(m0, 2048)], kerns[i - 1][pl.ds(m0, 2048), :], preferred_element_type=F32
                )
            return acc

        acc = lax.fori_loop(0, ctrs // 2048, block, jnp.zeros((tgt, pch), F32))
        if i == 1:
            pl.semaphore_wait(barrier, len(peers))
        if i > 0:
            fits[ctr, i - 1] = acc.astype(BF16)
            for d in range(1, GROUPS):
                fit_copy(i - 1, d).start()

    def fitted(i):
        for d in range(1, GROUPS):
            fit_copy(i, d).wait()
        total = fits[0, i].astype(F32)
        for g in range(1, GROUPS):
            total = total + fits[g, i].astype(F32)
        return total.astype(BF16)

    def rs_copy(c, d):
        return send(
            col.at[c, (mine + d) % PLANE], rsb.at[c, mine], rs_s.at[c, d], rs_r.at[c, d], plane_peer(d)
        )

    def z_copy(c, d):
        return send(zb.at[c, z], zb.at[c, z], z_s.at[c, d], z_r.at[c, d], z_peer(d))

    def ag_copy(c, d):
        return send(
            agb.at[c, mine], agb.at[c, mine], ag_s.at[c, d], ag_r.at[c, d], plane_peer(d)
        )

    def col_part(c, i, fit):
        return lax.dot_general(
            fit, kerns[i][c * mch : (c + 1) * mch, :], (((1,), (1,)), ((), ())), preferred_element_type=F32
        )

    def summed(ref, c, count):
        total = ref[c, 0]
        for k in range(1, count):
            total = total + ref[c, k]
        return total

    def to_rs(c, part):
        for j in range(PLANE):
            col[c, j] = part[:, j * LANES : (j + 1) * LANES]
        for d in range(1, PLANE):
            rs_copy(c, d).start()
        rsb[c, mine] = col[c, mine]

    def to_z(c):
        for d in range(1, PLANE):
            rs_copy(c, d).wait()
        zb[c, z] = summed(rsb, c, PLANE)
        for d in range(1, DEPTH):
            z_copy(c, d).start()

    def to_ag(c):
        for d in range(1, DEPTH):
            z_copy(c, d).wait()
        agb[c, mine] = summed(zb, c, DEPTH)
        for d in range(1, PLANE):
            ag_copy(c, d).start()

    fit = [fitted(i) for i in range(PCH - 1)]
    for c in range(EARLY):
        early[c] = sum((col_part(c, i, fit[i]) for i in range(1, PCH - 1)), col_part(c, 0, fit[0]))
    fit.append(fitted(PCH - 1))
    for c in range(EARLY):
        to_rs(c, early[c] + col_part(c, PCH - 1, fit[-1]))
    for c in range(EARLY, MCH):
        to_rs(c, sum((col_part(c, i, fit[i]) for i in range(1, PCH)), col_part(c, 0, fit[0])))
        if c == MCH - 2:
            to_z(0)
    to_z(1)
    to_z(2)
    to_ag(0)
    to_z(3)
    to_ag(1)
    to_ag(2)
    to_ag(3)

    scale = 2048.0 / (npts * DEPTH * PLANE)
    loads[3].wait()
    loads[4].wait()

    def finish(c, sums):
        for d in range(1, PLANE):
            ag_copy(c, d).wait()
        rr, rq, qq, dq = sums
        for k in range(PLANE):
            at = pl.ds(pl.multiple_of(c * mch + k * LANES, LANES), LANES)
            dirv, resv, prec = dir_ref[:, at], res_ref[:, at], prec_ref[:, at]
            image = agb[c, k] * scale + 0.5 * dirv
            q_ref[:, at] = image
            pr = prec * resv
            rr = rr + pr * resv
            rq = rq + pr * image
            qq = qq + prec * image * image
            dq = dq + dirv * image
        return rr, rq, qq, dq

    zero = jnp.zeros((tgt, LANES), F32)
    sums = lax.fori_loop(0, MCH, finish, (zero, zero, zero, zero))
    for k, v in enumerate(sums):
        scb[ctr, k] = v

    def sc_copy(d):
        return send(scb.at[ctr], scb.at[ctr], sc_s.at[d], sc_r.at[d], ctr_peer(d))

    for d in range(1, GROUPS):
        sc_copy(d).start()
    for d in range(1, GROUPS):
        sc_copy(d).wait()
    rr, rq, qq, dq = [
        jnp.sum(scb[0, k] + scb[1, k] + scb[2, k] + scb[3, k], axis=1, keepdims=True)
        for k in range(4)
    ]
    alpha = rr / dq
    rz_new = rr - 2.0 * alpha * rq + alpha * alpha * qq
    scal_ref[0] = jnp.broadcast_to(alpha, (tgt, LANES))
    scal_ref[1] = jnp.broadcast_to(rz_new / rr, (tgt, LANES))


def update(scal_ref, q_ref, coef_ref, res_ref, dir_ref, prec_ref, coef_out, res_out, dir_out):
    alpha, beta = scal_ref[0][:, :1], scal_ref[1][:, :1]
    dirv = dir_ref[...]
    res = res_ref[...] - alpha * q_ref[...]
    coef_out[...] = coef_ref[...] + alpha * dirv
    res_out[...] = res
    dir_out[...] = prec_ref[...] * res + beta * dirv


def shards(points, centres, coef, resid, direction, precond):
    tgt, ctrs = direction.shape
    npts = points.shape[1]
    prec = precond[None, :]
    vm = pl.BlockSpec(memory_space=pltpu.VMEM)
    dma = pltpu.SemaphoreType.DMA
    share = (tgt, LANES)
    whole = jax.ShapeDtypeStruct((tgt, ctrs), F32)
    args = (points, centres, direction, resid, prec)
    image, scal = pl.pallas_call(
        kernel,
        out_shape=(whole, jax.ShapeDtypeStruct((2, *share), F32)),
        in_specs=[pl.BlockSpec(memory_space=pl.ANY)] * 5,
        out_specs=(vm, vm),
        scratch_shapes=[
            *[pltpu.VMEM(a.shape, a.dtype) for a in args],
            pltpu.VMEM((128, npts), BF16),
            pltpu.VMEM((ctrs, 128), BF16),
            pltpu.VMEM((tgt, ctrs), BF16),
            *[pltpu.VMEM((ctrs, npts // PCH), BF16)] * PCH,
            pltpu.VMEM((GROUPS, PCH, tgt, npts // PCH), BF16),
            pltpu.VMEM((EARLY, tgt, ctrs // MCH), F32),
            pltpu.VMEM((MCH, PLANE, *share), F32),
            pltpu.VMEM((MCH, PLANE, *share), F32),
            pltpu.VMEM((MCH, DEPTH, *share), F32),
            pltpu.VMEM((MCH, PLANE, *share), F32),
            pltpu.VMEM((GROUPS, 4, *share), F32),
            dma((5,)),
            dma((PCH, GROUPS)), dma((PCH, GROUPS)),
            dma((MCH, PLANE)), dma((MCH, PLANE)),
            dma((MCH, DEPTH)), dma((MCH, DEPTH)),
            dma((MCH, PLANE)), dma((MCH, PLANE)),
            dma((GROUPS,)), dma((GROUPS,)),
        ],
        compiler_params=pltpu.CompilerParams(
            collective_id=0, has_side_effects=True, vmem_limit_bytes=48 << 20
        ),
        name="cg_step",
    )(*args)
    return pl.pallas_call(
        update,
        out_shape=(whole,) * 3,
        in_specs=[vm] * 6,
        out_specs=(vm,) * 3,
        compiler_params=pltpu.CompilerParams(vmem_limit_bytes=8 << 20),
        name="update",
    )(scal, image, coef, resid, direction, prec)


def solution(mesh):
    return jax.shard_map(
        shards,
        mesh=mesh,
        in_specs=(P(None, "pts"), *[P(None, "ctr")] * 4, P("ctr")),
        out_specs=(P(None, "ctr"),) * 3,
        check_vma=False,
    )
```

```python
import functools
import math

import jax
import jax.numpy as jnp
from jax import lax
from jax.experimental import pallas as pl
from jax.experimental.pallas import tpu as pltpu
from jax.sharding import PartitionSpec as P

MESH = pl.DeviceIdType.MESH
F32 = jnp.float32
BF16 = jnp.bfloat16
LOG2E = math.log2(math.e)

GROUPS = 4
PLANE = 16
DEPTH = 12
STRIDE = 3
PCH = 4
MCH = 4
EARLY = 2
UCH = 2
LANES = 128


def three_terms(v):
    hi = v.astype(BF16)
    rest = v - hi.astype(F32)
    mid = rest.astype(BF16)
    lo = (rest - mid.astype(F32)).astype(BF16)
    return hi, mid, lo


def tail_rows(width, first, second):
    row = lax.broadcasted_iota(jnp.int32, (32, width), 0)
    out = jnp.zeros((32, width), F32)
    for k, v in enumerate((*first, *second)):
        out = jnp.where(row == k, v if isinstance(v, float) else v.astype(F32), out)
    return out.astype(BF16)


def kernel(
    pts_hbm, cen_hbm, dir_hbm, res_hbm, prec_hbm, q_hbm, scal_ref,
    pts_ref, cen_ref, dir_ref, res_ref, prec_ref, q_ref,
    xa, ca, dirb, kern0, kern1, kern2, kern3, fits, early, col, rsb, z1b, z2b, agb, scb, spb,
    in_s, out_s, fit_s, fit_r, rs_s, rs_r, z1_s, z1_r, z2_s, z2_r, ag_s, ag_r, sc_s, sc_r, sp_s, sp_r,
):
    npts = pts_ref.shape[1]
    tgt, ctrs = dir_ref.shape
    pch = npts // PCH
    mch = ctrs // MCH
    kerns = (kern0, kern1, kern2, kern3)
    pts = lax.axis_index("pts")
    ctr = lax.axis_index("ctr")
    z = pts // PLANE
    mine = pts % PLANE
    third, step = z // STRIDE, z % STRIDE

    loads = [
        pltpu.make_async_copy(src, dst, in_s.at[k])
        for k, (src, dst) in enumerate(
            [(pts_hbm, pts_ref), (cen_hbm, cen_ref), (dir_hbm, dir_ref), (res_hbm, res_ref), (prec_hbm, prec_ref)]
        )
    ]
    for load in loads:
        load.start()

    def ctr_peer(d):
        return {"ctr": (ctr + d) % GROUPS}

    def plane_peer(d):
        return {"pts": z * PLANE + (mine + d) % PLANE}

    def z_peer(d):
        return {"pts": (z + d) % DEPTH * PLANE + mine}

    barrier = pltpu.get_barrier_semaphore()
    peers = [ctr_peer(d) for d in range(1, GROUPS)]
    peers += [plane_peer(d) for d in range(1, PLANE)]
    peers += [z_peer(d) for d in (3, 6, 9, 1, 11)]
    for peer in peers:
        pl.semaphore_signal(barrier, inc=1, device_id=peer, device_id_type=MESH)

    def send(src, dst, s, r, peer):
        return pltpu.make_async_remote_copy(
            src_ref=src, dst_ref=dst, send_sem=s, recv_sem=r, device_id=peer, device_id_type=MESH
        )

    loads[0].wait()
    x32 = pts_ref[...].astype(F32)
    hi, mid, lo = three_terms(x32 * (0.25 * LOG2E))
    xa[0:32, :] = hi
    xa[32:64, :] = mid
    xa[64:96, :] = lo
    xsq = jnp.sum(x32 * x32, axis=0, keepdims=True) * (-0.125 * LOG2E)
    xa[96:128, :] = tail_rows(npts, (1.0, 1.0, 1.0), three_terms(xsq))
    loads[1].wait()
    loads[2].wait()

    def centre_block(k, carry):
        m0 = pl.multiple_of(k * 1024, 1024)
        c = cen_ref[:, pl.ds(m0, 1024)]
        c32 = c.astype(F32)
        csq = jnp.sum(c32 * c32, axis=0, keepdims=True) * (-0.125 * LOG2E)
        tail = tail_rows(1024, three_terms(csq), (1.0, 1.0, 1.0))
        ca[pl.ds(m0, 1024), :] = jnp.concatenate([c, c, c, tail], axis=0).T
        dirb[:, pl.ds(m0, 1024)] = dir_ref[:, pl.ds(m0, 1024)].astype(BF16)
        return carry

    lax.fori_loop(0, ctrs // 1024, centre_block, 0)

    def fit_copy(i, d):
        return send(
            fits.at[ctr, i], fits.at[ctr, i], fit_s.at[i, d], fit_r.at[i, d], ctr_peer(d)
        )

    for i in range(PCH + 1):
        if i < PCH:
            s = jnp.dot(ca[...], xa[:, i * pch : (i + 1) * pch], preferred_element_type=F32)
            kerns[i][...] = jnp.exp2(s).astype(BF16)
        if i > 0:
            part = jnp.dot(dirb[...], kerns[i - 1][...], preferred_element_type=F32)
        if i == 1:
            pl.semaphore_wait(barrier, len(peers))
        if i > 0:
            fits[ctr, i - 1] = part.astype(BF16)
            for d in range(1, GROUPS):
                fit_copy(i - 1, d).start()

    def fitted(i):
        for d in range(1, GROUPS):
            fit_copy(i, d).wait()
        total = fits[0, i].astype(F32)
        for g in range(1, GROUPS):
            total = total + fits[g, i].astype(F32)
        return total.astype(BF16)

    def rs_copy(c, d):
        return send(
            col.at[c, (mine + d) % PLANE], rsb.at[c, mine], rs_s.at[c, d], rs_r.at[c, d], plane_peer(d)
        )

    def z1_copy(c, d):
        return send(
            z1b.at[c, third], z1b.at[c, third], z1_s.at[c, d], z1_r.at[c, d], z_peer(d * STRIDE)
        )

    def z2_copy(c, d):
        return send(
            z2b.at[c, step], z2b.at[c, step], z2_s.at[c, d], z2_r.at[c, d], z_peer((1, DEPTH - 1)[d])
        )

    def ag_copy(c, d):
        return send(
            agb.at[c, mine], agb.at[c, mine], ag_s.at[c, d], ag_r.at[c, d], plane_peer(d)
        )

    def col_part(c, i, fit):
        return lax.dot_general(
            fit, kerns[i][c * mch : (c + 1) * mch, :], (((1,), (1,)), ((), ())), preferred_element_type=F32
        )

    def summed(ref, c, count):
        total = ref[c, 0]
        for k in range(1, count):
            total = total + ref[c, k]
        return total

    def to_rs(c, part):
        for j in range(PLANE):
            col[c, j] = part[:, j * LANES : (j + 1) * LANES]
        for d in range(1, PLANE):
            rs_copy(c, d).start()
        rsb[c, mine] = col[c, mine]

    def to_z1(c):
        for d in range(1, PLANE):
            rs_copy(c, d).wait()
        z1b[c, third] = summed(rsb, c, PLANE)
        for d in range(1, DEPTH // STRIDE):
            z1_copy(c, d).start()

    def to_z2(c):
        for d in range(1, DEPTH // STRIDE):
            z1_copy(c, d).wait()
        z2b[c, step] = summed(z1b, c, DEPTH // STRIDE)
        for d in range(2):
            z2_copy(c, d).start()

    scale = 2048.0 / (npts * DEPTH * PLANE)

    def to_ag(c, sums):
        for d in range(2):
            z2_copy(c, d).wait()
        share = summed(z2b, c, STRIDE)
        agb[c, mine] = share
        for d in range(1, PLANE):
            ag_copy(c, d).start()
        at = pl.ds(pl.multiple_of(c * mch + mine * LANES, LANES), LANES)
        dirv, resv, prec = dir_ref[:, at], res_ref[:, at], prec_ref[:, at]
        image = share * scale + 0.5 * dirv
        pr = prec * resv
        new = (pr * resv, pr * image, prec * image * image, dirv * image)
        return [a + b for a, b in zip(sums, new)]

    fit = [fitted(i) for i in range(PCH - 1)]
    for c in range(EARLY):
        early[c] = sum((col_part(c, i, fit[i]) for i in range(1, PCH - 1)), col_part(c, 0, fit[0]))
    fit.append(fitted(PCH - 1))
    for c in range(EARLY):
        to_rs(c, early[c] + col_part(c, PCH - 1, fit[-1]))
    for c in range(EARLY, MCH):
        to_rs(c, sum((col_part(c, i, fit[i]) for i in range(1, PCH)), col_part(c, 0, fit[0])))
        if c == MCH - 2:
            to_z1(0)
    loads[3].wait()
    loads[4].wait()
    sums = [jnp.zeros((tgt, LANES), F32)] * 4
    to_z1(1)
    to_z2(0)
    to_z1(2)
    to_z2(1)
    sums = to_ag(0, sums)
    to_z1(3)
    to_z2(2)
    sums = to_ag(1, sums)
    to_z2(3)
    sums = to_ag(2, sums)
    sums = to_ag(3, sums)

    lane = lax.broadcasted_iota(jnp.int32, (tgt, LANES), 1)
    packed = jnp.zeros((tgt, LANES), F32)
    for k, v in enumerate(sums):
        packed = jnp.where(lane == k, jnp.sum(v, axis=1, keepdims=True), packed)
    scb[ctr] = packed

    def sc_copy(d):
        return send(scb.at[ctr], scb.at[ctr], sc_s.at[d], sc_r.at[d], ctr_peer(d))

    def sp_copy(d):
        return send(spb.at[mine], spb.at[mine], sp_s.at[d], sp_r.at[d], plane_peer(d))

    for d in range(1, GROUPS):
        sc_copy(d).start()
    for d in range(1, GROUPS):
        sc_copy(d).wait()
    spb[mine] = scb[0] + scb[1] + scb[2] + scb[3]
    for d in range(1, PLANE):
        sp_copy(d).start()

    def out_copy(c):
        at = pl.ds(pl.multiple_of(c * mch, mch), mch)
        return pltpu.make_async_copy(q_ref.at[:, at], q_hbm.at[:, at], out_s.at[c])

    def finish(c, carry):
        for d in range(1, PLANE):
            ag_copy(c, d).wait()
        for k in range(PLANE):
            at = pl.ds(pl.multiple_of(c * mch + k * LANES, LANES), LANES)
            q_ref[:, at] = agb[c, k] * scale + 0.5 * dir_ref[:, at]
        out_copy(c).start()
        return carry

    lax.fori_loop(0, MCH, finish, 0)
    for d in range(1, PLANE):
        sp_copy(d).wait()
    packed = spb[0]
    for k in range(1, PLANE):
        packed = packed + spb[k]
    rr, rq, qq, dq = [
        jnp.sum(jnp.where(lane == k, packed, 0.0), axis=1, keepdims=True) for k in range(4)
    ]
    alpha = rr / dq
    rz_new = rr - 2.0 * alpha * rq + alpha * alpha * qq
    scal_ref[0] = jnp.broadcast_to(alpha, (tgt, LANES))
    scal_ref[1] = jnp.broadcast_to(rz_new / rr, (tgt, LANES))
    for c in range(MCH):
        out_copy(c).wait()


def update(scal_ref, q_ref, coef_ref, res_ref, dir_ref, prec_ref, coef_out, res_out, dir_out):
    alpha, beta = scal_ref[0][:, :1], scal_ref[1][:, :1]
    dirv = dir_ref[...]
    res = res_ref[...] - alpha * q_ref[...]
    coef_out[...] = coef_ref[...] + alpha * dirv
    res_out[...] = res
    dir_out[...] = prec_ref[...] * res + beta * dirv


def shards(points, centres, coef, resid, direction, precond):
    tgt, ctrs = direction.shape
    npts = points.shape[1]
    prec = precond[None, :]
    vm = pl.BlockSpec(memory_space=pltpu.VMEM)
    dma = pltpu.SemaphoreType.DMA
    share = (tgt, LANES)
    whole = jax.ShapeDtypeStruct((tgt, ctrs), F32)
    args = (points, centres, direction, resid, prec)
    image, scal = pl.pallas_call(
        kernel,
        out_shape=(whole, jax.ShapeDtypeStruct((2, *share), F32)),
        in_specs=[pl.BlockSpec(memory_space=pl.ANY)] * 5,
        out_specs=(pl.BlockSpec(memory_space=pl.ANY), vm),
        scratch_shapes=[
            *[pltpu.VMEM(a.shape, a.dtype) for a in args],
            pltpu.VMEM((tgt, ctrs), F32),
            pltpu.VMEM((128, npts), BF16),
            pltpu.VMEM((ctrs, 128), BF16),
            pltpu.VMEM((tgt, ctrs), BF16),
            *[pltpu.VMEM((ctrs, npts // PCH), BF16)] * PCH,
            pltpu.VMEM((GROUPS, PCH, tgt, npts // PCH), BF16),
            pltpu.VMEM((EARLY, tgt, ctrs // MCH), F32),
            pltpu.VMEM((MCH, PLANE, *share), F32),
            pltpu.VMEM((MCH, PLANE, *share), F32),
            pltpu.VMEM((MCH, DEPTH // STRIDE, *share), F32),
            pltpu.VMEM((MCH, STRIDE, *share), F32),
            pltpu.VMEM((MCH, PLANE, *share), F32),
            pltpu.VMEM((GROUPS, *share), F32),
            pltpu.VMEM((PLANE, *share), F32),
            dma((5,)),
            dma((MCH,)),
            dma((PCH, GROUPS)), dma((PCH, GROUPS)),
            dma((MCH, PLANE)), dma((MCH, PLANE)),
            dma((MCH, DEPTH // STRIDE)), dma((MCH, DEPTH // STRIDE)),
            dma((MCH, 2)), dma((MCH, 2)),
            dma((MCH, PLANE)), dma((MCH, PLANE)),
            dma((GROUPS,)), dma((GROUPS,)),
            dma((PLANE,)), dma((PLANE,)),
        ],
        compiler_params=pltpu.CompilerParams(
            collective_id=0, has_side_effects=True, vmem_limit_bytes=56 << 20
        ),
        name="cg_step",
    )(*args)
    return pl.pallas_call(
        update,
        out_shape=(whole,) * 3,
        grid=(UCH,),
        in_specs=[
            pl.BlockSpec((2, *share), lambda k: (0, 0, 0)),
            *[pl.BlockSpec((tgt, ctrs // UCH), lambda k: (0, k))] * 4,
            pl.BlockSpec((1, ctrs // UCH), lambda k: (0, k)),
        ],
        out_specs=(pl.BlockSpec((tgt, ctrs // UCH), lambda k: (0, k)),) * 3,
        compiler_params=pltpu.CompilerParams(vmem_limit_bytes=60 << 20),
        name="update",
    )(scal, image, coef, resid, direction, prec)


def solution(mesh):
    return jax.shard_map(
        shards,
        mesh=mesh,
        in_specs=(P(None, "pts"), *[P(None, "ctr")] * 4, P("ctr")),
        out_specs=(P(None, "ctr"),) * 3,
        check_vma=False,
    )
```

```python
import functools
import math

import jax
import jax.numpy as jnp
from jax import lax
from jax.experimental import pallas as pl
from jax.experimental.pallas import tpu as pltpu
from jax.sharding import PartitionSpec as P

MESH = pl.DeviceIdType.MESH
F32 = jnp.float32
BF16 = jnp.bfloat16
LOG2E = math.log2(math.e)

GROUPS = 4
PLANE = 16
DEPTH = 12
STRIDE = 3
PCH = 4
MCH = 4
EARLY = 2
UCH = 2
LANES = 128


def three_terms(v):
    hi = v.astype(BF16)
    rest = v - hi.astype(F32)
    mid = rest.astype(BF16)
    lo = (rest - mid.astype(F32)).astype(BF16)
    return hi, mid, lo


def tail_rows(width, first, second):
    row = lax.broadcasted_iota(jnp.int32, (32, width), 0)
    out = jnp.zeros((32, width), F32)
    for k, v in enumerate((*first, *second)):
        out = jnp.where(row == k, v if isinstance(v, float) else v.astype(F32), out)
    return out.astype(BF16)


def kernel(
    pts_hbm, cen_hbm, dir_hbm, res_hbm, prec_hbm, q_hbm, scal_ref,
    pts_ref, cen_ref, dir_ref, res_ref, prec_ref, q_ref,
    xa, ca, dirb, kern0, kern1, kern2, kern3, fits, early, col, rsb, z1b, z2b, agb, scb, spb,
    in_s, out_s, fit_s, fit_r, rs_s, rs_r, z1_s, z1_r, z2_s, z2_r, ag_s, ag_r, sc_s, sc_r, sp_s, sp_r,
):
    npts = pts_ref.shape[1]
    tgt, ctrs = dir_ref.shape
    pch = npts // PCH
    mch = ctrs // MCH
    kerns = (kern0, kern1, kern2, kern3)
    pts = lax.axis_index("pts")
    ctr = lax.axis_index("ctr")
    z = pts // PLANE
    mine = pts % PLANE
    third, step = z // STRIDE, z % STRIDE

    loads = [
        pltpu.make_async_copy(src, dst, in_s.at[k])
        for k, (src, dst) in enumerate(
            [(pts_hbm, pts_ref), (cen_hbm, cen_ref), (dir_hbm, dir_ref), (res_hbm, res_ref), (prec_hbm, prec_ref)]
        )
    ]
    for load in loads:
        load.start()

    def ctr_peer(d):
        return {"ctr": (ctr + d) % GROUPS}

    def plane_peer(d):
        return {"pts": z * PLANE + (mine + d) % PLANE}

    def z_peer(d):
        return {"pts": (z + d) % DEPTH * PLANE + mine}

    barrier = pltpu.get_barrier_semaphore()
    peers = [ctr_peer(d) for d in range(1, GROUPS)]
    peers += [plane_peer(d) for d in range(1, PLANE)]
    peers += [z_peer(d) for d in (3, 6, 9, 1, 11)]
    for peer in peers:
        pl.semaphore_signal(barrier, inc=1, device_id=peer, device_id_type=MESH)

    def send(src, dst, s, r, peer):
        return pltpu.make_async_remote_copy(
            src_ref=src, dst_ref=dst, send_sem=s, recv_sem=r, device_id=peer, device_id_type=MESH
        )

    loads[0].wait()
    x32 = pts_ref[...].astype(F32)
    hi, mid, lo = three_terms(x32 * (0.25 * LOG2E))
    xa[0:32, :] = hi
    xa[32:64, :] = mid
    xa[64:96, :] = lo
    xsq = jnp.sum(x32 * x32, axis=0, keepdims=True) * (-0.125 * LOG2E)
    xa[96:128, :] = tail_rows(npts, (1.0, 1.0, 1.0), three_terms(xsq))
    loads[1].wait()
    loads[2].wait()

    def centre_block(k, carry):
        m0 = pl.multiple_of(k * 1024, 1024)
        c = cen_ref[:, pl.ds(m0, 1024)]
        c32 = c.astype(F32)
        csq = jnp.sum(c32 * c32, axis=0, keepdims=True) * (-0.125 * LOG2E)
        tail = tail_rows(1024, three_terms(csq), (1.0, 1.0, 1.0))
        ca[pl.ds(m0, 1024), :] = jnp.concatenate([c, c, c, tail], axis=0).T
        dirb[:, pl.ds(m0, 1024)] = dir_ref[:, pl.ds(m0, 1024)].astype(BF16)
        return carry

    lax.fori_loop(0, ctrs // 1024, centre_block, 0)

    def fit_copy(i, d):
        return send(
            fits.at[ctr, i], fits.at[ctr, i], fit_s.at[i, d], fit_r.at[i, d], ctr_peer(d)
        )

    for i in range(PCH + 1):
        if i < PCH:
            s = jnp.dot(ca[...], xa[:, i * pch : (i + 1) * pch], preferred_element_type=F32)
            kerns[i][...] = jnp.exp2(s).astype(BF16)
        if i > 0:
            part = jnp.dot(dirb[...], kerns[i - 1][...], preferred_element_type=F32)
        if i == 1:
            pl.semaphore_wait(barrier, len(peers))
        if i > 0:
            fits[ctr, i - 1] = part.astype(BF16)
            for d in range(1, GROUPS):
                fit_copy(i - 1, d).start()

    def fitted(i):
        for d in range(1, GROUPS):
            fit_copy(i, d).wait()
        total = fits[0, i].astype(F32)
        for g in range(1, GROUPS):
            total = total + fits[g, i].astype(F32)
        return total.astype(BF16)

    def rs_copy(c, d):
        return send(
            col.at[c, (mine + d) % PLANE], rsb.at[c, mine], rs_s.at[c, d], rs_r.at[c, d], plane_peer(d)
        )

    def z1_copy(c, d):
        return send(
            z1b.at[c, third], z1b.at[c, third], z1_s.at[c, d], z1_r.at[c, d], z_peer(d * STRIDE)
        )

    def z2_copy(c, d):
        return send(
            z2b.at[c, step], z2b.at[c, step], z2_s.at[c, d], z2_r.at[c, d], z_peer((1, DEPTH - 1)[d])
        )

    def ag_copy(c, d):
        return send(
            agb.at[c, mine], agb.at[c, mine], ag_s.at[c, d], ag_r.at[c, d], plane_peer(d)
        )

    def col_part(c, i, fit):
        return lax.dot_general(
            fit, kerns[i][c * mch : (c + 1) * mch, :], (((1,), (1,)), ((), ())), preferred_element_type=F32
        )

    def summed(ref, c, count):
        total = ref[c, 0]
        for k in range(1, count):
            total = total + ref[c, k]
        return total

    def to_rs(c, part):
        for j in range(PLANE):
            col[c, j] = part[:, j * LANES : (j + 1) * LANES]
        for d in range(1, PLANE):
            rs_copy(c, d).start()
        rsb[c, mine] = col[c, mine]

    def to_z1(c):
        for d in range(1, PLANE):
            rs_copy(c, d).wait()
        z1b[c, third] = summed(rsb, c, PLANE)
        for d in range(1, DEPTH // STRIDE):
            z1_copy(c, d).start()

    def to_z2(c):
        for d in range(1, DEPTH // STRIDE):
            z1_copy(c, d).wait()
        z2b[c, step] = summed(z1b, c, DEPTH // STRIDE)
        for d in range(2):
            z2_copy(c, d).start()

    scale = 2048.0 / (npts * DEPTH * PLANE)

    def start_ag(c):
        for d in range(1, PLANE):
            ag_copy(c, d).start()

    def to_ag(c, sums):
        for d in range(2):
            z2_copy(c, d).wait()
        share = summed(z2b, c, STRIDE)
        agb[c, mine] = share
        if c < MCH - 1:
            start_ag(c)
        at = pl.ds(pl.multiple_of(c * mch + mine * LANES, LANES), LANES)
        dirv, resv, prec = dir_ref[:, at], res_ref[:, at], prec_ref[:, at]
        image = share * scale + 0.5 * dirv
        pr = prec * resv
        new = (pr * resv, pr * image, prec * image * image, dirv * image)
        return [a + b for a, b in zip(sums, new)]

    fit = [fitted(i) for i in range(PCH - 1)]
    for c in range(EARLY):
        early[c] = sum((col_part(c, i, fit[i]) for i in range(1, PCH - 1)), col_part(c, 0, fit[0]))
    fit.append(fitted(PCH - 1))
    for c in range(EARLY):
        to_rs(c, early[c] + col_part(c, PCH - 1, fit[-1]))
    for c in range(EARLY, MCH):
        to_rs(c, sum((col_part(c, i, fit[i]) for i in range(1, PCH)), col_part(c, 0, fit[0])))
        if c == MCH - 2:
            to_z1(0)
    loads[3].wait()
    loads[4].wait()
    sums = [jnp.zeros((tgt, LANES), F32)] * 4
    to_z1(1)
    to_z2(0)
    to_z1(2)
    to_z2(1)
    sums = to_ag(0, sums)
    to_z1(3)
    to_z2(2)
    sums = to_ag(1, sums)
    to_z2(3)
    sums = to_ag(2, sums)
    sums = to_ag(3, sums)

    lane = lax.broadcasted_iota(jnp.int32, (tgt, LANES), 1)
    spot = lane - lax.broadcasted_iota(jnp.int32, (tgt, LANES), 0)
    packed = jnp.zeros((tgt, LANES), F32)
    for k, v in enumerate(sums):
        packed = jnp.where(spot == k * tgt, jnp.sum(v, axis=1, keepdims=True), packed)
    spb[mine] = jnp.sum(packed, axis=0, keepdims=True)

    def sp_copy(d):
        return send(spb.at[mine], spb.at[mine], sp_s.at[d], sp_r.at[d], plane_peer(d))

    def sc_copy(d):
        return send(scb.at[ctr], scb.at[ctr], sc_s.at[d], sc_r.at[d], ctr_peer(d))

    for d in range(1, PLANE):
        sp_copy(d).start()
    start_ag(MCH - 1)
    for d in range(1, PLANE):
        sp_copy(d).wait()
    total = spb[0]
    for k in range(1, PLANE):
        total = total + spb[k]
    scb[ctr] = total
    for d in range(1, GROUPS):
        sc_copy(d).start()

    def out_copy(c):
        at = pl.ds(pl.multiple_of(c * mch, mch), mch)
        return pltpu.make_async_copy(q_ref.at[:, at], q_hbm.at[:, at], out_s.at[c])

    def finish(c, carry):
        for d in range(1, PLANE):
            ag_copy(c, d).wait()
        for k in range(PLANE):
            at = pl.ds(pl.multiple_of(c * mch + k * LANES, LANES), LANES)
            q_ref[:, at] = agb[c, k] * scale + 0.5 * dir_ref[:, at]
        out_copy(c).start()
        return carry

    lax.fori_loop(0, MCH, finish, 0)
    for d in range(1, GROUPS):
        sc_copy(d).wait()
    total = scb[0] + scb[1] + scb[2] + scb[3]
    rr, rq, qq, dq = [
        jnp.sum(jnp.where(spot == k * tgt, total, 0.0), axis=1, keepdims=True) for k in range(4)
    ]
    alpha = rr / dq
    rz_new = rr - 2.0 * alpha * rq + alpha * alpha * qq
    scal_ref[0] = jnp.broadcast_to(alpha, (tgt, LANES))
    scal_ref[1] = jnp.broadcast_to(rz_new / rr, (tgt, LANES))
    for c in range(MCH):
        out_copy(c).wait()


def update(scal_ref, q_ref, coef_ref, res_ref, dir_ref, prec_ref, coef_out, res_out, dir_out):
    alpha, beta = scal_ref[0][:, :1], scal_ref[1][:, :1]
    dirv = dir_ref[...]
    res = res_ref[...] - alpha * q_ref[...]
    coef_out[...] = coef_ref[...] + alpha * dirv
    res_out[...] = res
    dir_out[...] = prec_ref[...] * res + beta * dirv


def shards(points, centres, coef, resid, direction, precond):
    tgt, ctrs = direction.shape
    npts = points.shape[1]
    prec = precond[None, :]
    vm = pl.BlockSpec(memory_space=pltpu.VMEM)
    dma = pltpu.SemaphoreType.DMA
    share = (tgt, LANES)
    whole = jax.ShapeDtypeStruct((tgt, ctrs), F32)
    args = (points, centres, direction, resid, prec)
    image, scal = pl.pallas_call(
        kernel,
        out_shape=(whole, jax.ShapeDtypeStruct((2, *share), F32)),
        in_specs=[pl.BlockSpec(memory_space=pl.ANY)] * 5,
        out_specs=(pl.BlockSpec(memory_space=pl.ANY), vm),
        scratch_shapes=[
            *[pltpu.VMEM(a.shape, a.dtype) for a in args],
            pltpu.VMEM((tgt, ctrs), F32),
            pltpu.VMEM((128, npts), BF16),
            pltpu.VMEM((ctrs, 128), BF16),
            pltpu.VMEM((tgt, ctrs), BF16),
            *[pltpu.VMEM((ctrs, npts // PCH), BF16)] * PCH,
            pltpu.VMEM((GROUPS, PCH, tgt, npts // PCH), BF16),
            pltpu.VMEM((EARLY, tgt, ctrs // MCH), F32),
            pltpu.VMEM((MCH, PLANE, *share), F32),
            pltpu.VMEM((MCH, PLANE, *share), F32),
            pltpu.VMEM((MCH, DEPTH // STRIDE, *share), F32),
            pltpu.VMEM((MCH, STRIDE, *share), F32),
            pltpu.VMEM((MCH, PLANE, *share), F32),
            pltpu.VMEM((GROUPS, 1, LANES), F32),
            pltpu.VMEM((PLANE, 1, LANES), F32),
            dma((5,)),
            dma((MCH,)),
            dma((PCH, GROUPS)), dma((PCH, GROUPS)),
            dma((MCH, PLANE)), dma((MCH, PLANE)),
            dma((MCH, DEPTH // STRIDE)), dma((MCH, DEPTH // STRIDE)),
            dma((MCH, 2)), dma((MCH, 2)),
            dma((MCH, PLANE)), dma((MCH, PLANE)),
            dma((GROUPS,)), dma((GROUPS,)),
            dma((PLANE,)), dma((PLANE,)),
        ],
        compiler_params=pltpu.CompilerParams(
            collective_id=0, has_side_effects=True, vmem_limit_bytes=56 << 20
        ),
        name="cg_step",
    )(*args)
    return pl.pallas_call(
        update,
        out_shape=(whole,) * 3,
        grid=(UCH,),
        in_specs=[
            pl.BlockSpec((2, *share), lambda k: (0, 0, 0)),
            *[pl.BlockSpec((tgt, ctrs // UCH), lambda k: (0, k))] * 4,
            pl.BlockSpec((1, ctrs // UCH), lambda k: (0, k)),
        ],
        out_specs=(pl.BlockSpec((tgt, ctrs // UCH), lambda k: (0, k)),) * 3,
        compiler_params=pltpu.CompilerParams(vmem_limit_bytes=60 << 20),
        name="update",
    )(scal, image, coef, resid, direction, prec)


def solution(mesh):
    return jax.shard_map(
        shards,
        mesh=mesh,
        in_specs=(P(None, "pts"), *[P(None, "ctr")] * 4, P("ctr")),
        out_specs=(P(None, "ctr"),) * 3,
        check_vma=False,
    )
```

```python
import functools
import math

import jax
import jax.numpy as jnp
from jax import lax
from jax.experimental import pallas as pl
from jax.experimental.pallas import tpu as pltpu
from jax.sharding import PartitionSpec as P

MESH = pl.DeviceIdType.MESH
F32 = jnp.float32
BF16 = jnp.bfloat16
LOG2E = math.log2(math.e)

GROUPS = 4
PLANE = 16
DEPTH = 12
STRIDE = 3
PCH = 4
MCH = 4
EARLY = 2
UCH = 2
LANES = 128
CROWS = 2048
IN_PLANE = (4, 12, 3, 5, 11, 13, 2, 6, 10, 14, 1, 7, 9, 15, 8)
ALONG_Z = (6, 5, 7, 4, 8, 3, 9, 2, 10, 1, 11)


def three_terms(v):
    hi = v.astype(BF16)
    rest = v - hi.astype(F32)
    mid = rest.astype(BF16)
    lo = (rest - mid.astype(F32)).astype(BF16)
    return hi, mid, lo


def tail_rows(width, first, second):
    row = lax.broadcasted_iota(jnp.int32, (32, width), 0)
    out = jnp.zeros((32, width), F32)
    for k, v in enumerate((*first, *second)):
        out = jnp.where(row == k, v if isinstance(v, float) else v.astype(F32), out)
    return out.astype(BF16)


def kernel(
    pts_hbm, cen_hbm, dir_hbm, res_hbm, prec_hbm, q_hbm, scal_ref,
    pts_ref, cen_ref, dir_ref, res_ref, prec_ref, q_ref,
    xa, ca, dirb, kern0, kern1, kern2, kern3, fits, early, col, rsb, z1b, z2b, zb, agb, scb, spb,
    in_s, out_s, fit_s, fit_r, rs_s, rs_r, z1_s, z1_r, z2_s, z2_r, z_s, z_r, ag_s, ag_r, sc_s, sc_r, sp_s, sp_r,
):
    npts = pts_ref.shape[1]
    tgt, ctrs = dir_ref.shape
    pch = npts // PCH
    mch = ctrs // MCH
    kerns = (kern0, kern1, kern2, kern3)
    pts = lax.axis_index("pts")
    ctr = lax.axis_index("ctr")
    z = pts // PLANE
    mine = pts % PLANE
    third, step = z // STRIDE, z % STRIDE

    loads = [
        pltpu.make_async_copy(src, dst, in_s.at[k])
        for k, (src, dst) in enumerate(
            [(pts_hbm, pts_ref), (cen_hbm, cen_ref), (dir_hbm, dir_ref), (res_hbm, res_ref), (prec_hbm, prec_ref)]
        )
    ]
    for load in loads:
        load.start()

    def ctr_peer(d):
        return {"ctr": (ctr + d) % GROUPS}

    def plane_peer(d):
        return {"pts": z * PLANE + (mine + d) % PLANE}

    def z_peer(d):
        return {"pts": (z + d) % DEPTH * PLANE + mine}

    barrier = pltpu.get_barrier_semaphore()
    peers = [ctr_peer(d) for d in range(1, GROUPS)]
    peers += [plane_peer(d) for d in range(1, PLANE)]
    peers += [z_peer(d) for d in ALONG_Z]
    for peer in peers:
        pl.semaphore_signal(barrier, inc=1, device_id=peer, device_id_type=MESH)

    def send(src, dst, s, r, peer):
        return pltpu.make_async_remote_copy(
            src_ref=src, dst_ref=dst, send_sem=s, recv_sem=r, device_id=peer, device_id_type=MESH
        )

    loads[0].wait()
    x32 = pts_ref[...].astype(F32)
    hi, mid, lo = three_terms(x32 * (0.25 * LOG2E))
    xa[0:32, :] = hi
    xa[32:64, :] = mid
    xa[64:96, :] = lo
    xsq = jnp.sum(x32 * x32, axis=0, keepdims=True) * (-0.125 * LOG2E)
    xa[96:128, :] = tail_rows(npts, (1.0, 1.0, 1.0), three_terms(xsq))
    loads[1].wait()
    loads[2].wait()

    def centre_block(k, rows):
        at = slice(k * rows, (k + 1) * rows)
        c = cen_ref[:, at]
        c32 = c.astype(F32)
        csq = jnp.sum(c32 * c32, axis=0, keepdims=True) * (-0.125 * LOG2E)
        tail = tail_rows(rows, three_terms(csq), (1.0, 1.0, 1.0))
        block = jnp.concatenate([c, c, c, tail], axis=0).T
        ca[at, :] = block
        dirb[:, at] = dir_ref[:, at].astype(BF16)
        s = jnp.dot(block, xa[:, :pch], preferred_element_type=F32)
        kerns[0][at, :] = jnp.exp2(s).astype(BF16)

    def fit_copy(i, d):
        return send(
            fits.at[ctr, i], fits.at[ctr, i], fit_s.at[i, d], fit_r.at[i, d], ctr_peer(d)
        )

    for i in range(PCH + 1):
        if i == 0:
            for k in range(ctrs // CROWS):
                centre_block(k, CROWS)
        elif i < PCH:
            s = jnp.dot(ca[...], xa[:, i * pch : (i + 1) * pch], preferred_element_type=F32)
            kerns[i][...] = jnp.exp2(s).astype(BF16)
        if i > 0:
            part = jnp.dot(dirb[...], kerns[i - 1][...], preferred_element_type=F32)
        if i == 1:
            pl.semaphore_wait(barrier, len(peers))
        if i > 0:
            fits[ctr, i - 1] = part.astype(BF16)
            for d in range(1, GROUPS):
                fit_copy(i - 1, d).start()

    def fitted(i):
        for d in range(1, GROUPS):
            fit_copy(i, d).wait()
        total = fits[0, i].astype(F32)
        for g in range(1, GROUPS):
            total = total + fits[g, i].astype(F32)
        return total.astype(BF16)

    def rs_copy(c, d):
        return send(
            col.at[c, (mine + d) % PLANE], rsb.at[c, mine], rs_s.at[c, d], rs_r.at[c, d], plane_peer(d)
        )

    def z1_copy(c, d):
        return send(
            z1b.at[c, third], z1b.at[c, third], z1_s.at[c, d], z1_r.at[c, d], z_peer(d * STRIDE)
        )

    def z2_copy(c, d):
        return send(
            z2b.at[c, step], z2b.at[c, step], z2_s.at[c, d], z2_r.at[c, d], z_peer((1, DEPTH - 1)[d])
        )

    def z_copy(d):
        return send(zb.at[z], zb.at[z], z_s.at[d], z_r.at[d], z_peer(d))

    def ag_copy(c, d):
        return send(
            agb.at[c, mine], agb.at[c, mine], ag_s.at[c, d], ag_r.at[c, d], plane_peer(d)
        )

    def col_part(c, i, fit):
        return lax.dot_general(
            fit, kerns[i][c * mch : (c + 1) * mch, :], (((1,), (1,)), ((), ())), preferred_element_type=F32
        )

    def summed(ref, c, count):
        total = ref[c, 0]
        for k in range(1, count):
            total = total + ref[c, k]
        return total

    def to_rs(c, part):
        for j in range(PLANE):
            col[c, j] = part[:, j * LANES : (j + 1) * LANES]
        for d in IN_PLANE:
            rs_copy(c, d).start()
        rsb[c, mine] = col[c, mine]

    def to_z1(c):
        for d in range(1, PLANE):
            rs_copy(c, d).wait()
        if c == MCH - 1:
            zb[z] = summed(rsb, c, PLANE)
            for d in ALONG_Z:
                z_copy(d).start()
            return
        z1b[c, third] = summed(rsb, c, PLANE)
        for d in (2, 1, 3):
            z1_copy(c, d).start()

    def to_z2(c):
        for d in range(1, DEPTH // STRIDE):
            z1_copy(c, d).wait()
        z2b[c, step] = summed(z1b, c, DEPTH // STRIDE)
        for d in range(2):
            z2_copy(c, d).start()

    scale = 2048.0 / (npts * DEPTH * PLANE)

    def start_ag(c):
        for d in IN_PLANE:
            ag_copy(c, d).start()

    def to_ag(c, sums):
        if c == MCH - 1:
            for d in ALONG_Z:
                z_copy(d).wait()
            share = zb[0]
            for k in range(1, DEPTH):
                share = share + zb[k]
        else:
            for d in range(2):
                z2_copy(c, d).wait()
            share = summed(z2b, c, STRIDE)
        agb[c, mine] = share
        if c < MCH - 1:
            start_ag(c)
        at = pl.ds(pl.multiple_of(c * mch + mine * LANES, LANES), LANES)
        dirv, resv, prec = dir_ref[:, at], res_ref[:, at], prec_ref[:, at]
        image = share * scale + 0.5 * dirv
        pr = prec * resv
        new = (pr * resv, pr * image, prec * image * image, dirv * image)
        return [a + b for a, b in zip(sums, new)]

    fit = [fitted(i) for i in range(PCH - 1)]
    for c in range(EARLY):
        early[c] = sum((col_part(c, i, fit[i]) for i in range(1, PCH - 1)), col_part(c, 0, fit[0]))
    fit.append(fitted(PCH - 1))
    for c in range(EARLY):
        to_rs(c, early[c] + col_part(c, PCH - 1, fit[-1]))
    for c in range(EARLY, MCH):
        to_rs(c, sum((col_part(c, i, fit[i]) for i in range(1, PCH)), col_part(c, 0, fit[0])))
        if c == MCH - 2:
            to_z1(0)
    loads[3].wait()
    loads[4].wait()
    sums = [jnp.zeros((tgt, LANES), F32)] * 4
    to_z1(1)
    to_z2(0)
    to_z1(2)
    to_z2(1)
    sums = to_ag(0, sums)
    to_z1(3)
    to_z2(2)
    sums = to_ag(1, sums)
    sums = to_ag(2, sums)
    sums = to_ag(3, sums)

    lane = lax.broadcasted_iota(jnp.int32, (tgt, LANES), 1)
    spot = lane - lax.broadcasted_iota(jnp.int32, (tgt, LANES), 0)
    packed = jnp.zeros((tgt, LANES), F32)
    for k, v in enumerate(sums):
        packed = jnp.where(spot == k * tgt, jnp.sum(v, axis=1, keepdims=True), packed)
    spb[mine] = jnp.sum(packed, axis=0, keepdims=True)

    def sp_copy(d):
        return send(spb.at[mine], spb.at[mine], sp_s.at[d], sp_r.at[d], plane_peer(d))

    def sc_copy(d):
        return send(scb.at[ctr], scb.at[ctr], sc_s.at[d], sc_r.at[d], ctr_peer(d))

    for d in IN_PLANE:
        sp_copy(d).start()
    start_ag(MCH - 1)
    for d in range(1, PLANE):
        sp_copy(d).wait()
    total = spb[0]
    for k in range(1, PLANE):
        total = total + spb[k]
    scb[ctr] = total
    for d in range(1, GROUPS):
        sc_copy(d).start()

    def out_copy(c):
        at = pl.ds(pl.multiple_of(c * mch, mch), mch)
        return pltpu.make_async_copy(q_ref.at[:, at], q_hbm.at[:, at], out_s.at[c])

    def finish(c, carry):
        for d in range(1, PLANE):
            ag_copy(c, d).wait()
        for k in range(PLANE):
            at = pl.ds(pl.multiple_of(c * mch + k * LANES, LANES), LANES)
            q_ref[:, at] = agb[c, k] * scale + 0.5 * dir_ref[:, at]
        out_copy(c).start()
        return carry

    lax.fori_loop(0, MCH, finish, 0)
    for d in range(1, GROUPS):
        sc_copy(d).wait()
    total = scb[0] + scb[1] + scb[2] + scb[3]
    rr, rq, qq, dq = [
        jnp.sum(jnp.where(spot == k * tgt, total, 0.0), axis=1, keepdims=True) for k in range(4)
    ]
    alpha = rr / dq
    rz_new = rr - 2.0 * alpha * rq + alpha * alpha * qq
    scal_ref[0] = jnp.broadcast_to(alpha, (tgt, LANES))
    scal_ref[1] = jnp.broadcast_to(rz_new / rr, (tgt, LANES))
    for c in range(MCH):
        out_copy(c).wait()


def update(scal_ref, q_ref, coef_ref, res_ref, dir_ref, prec_ref, coef_out, res_out, dir_out):
    alpha, beta = scal_ref[0][:, :1], scal_ref[1][:, :1]
    dirv = dir_ref[...]
    res = res_ref[...] - alpha * q_ref[...]
    coef_out[...] = coef_ref[...] + alpha * dirv
    res_out[...] = res
    dir_out[...] = prec_ref[...] * res + beta * dirv


def shards(points, centres, coef, resid, direction, precond):
    tgt, ctrs = direction.shape
    npts = points.shape[1]
    prec = precond[None, :]
    vm = pl.BlockSpec(memory_space=pltpu.VMEM)
    dma = pltpu.SemaphoreType.DMA
    share = (tgt, LANES)
    whole = jax.ShapeDtypeStruct((tgt, ctrs), F32)
    args = (points, centres, direction, resid, prec)
    image, scal = pl.pallas_call(
        kernel,
        out_shape=(whole, jax.ShapeDtypeStruct((2, *share), F32)),
        in_specs=[pl.BlockSpec(memory_space=pl.ANY)] * 5,
        out_specs=(pl.BlockSpec(memory_space=pl.ANY), vm),
        scratch_shapes=[
            *[pltpu.VMEM(a.shape, a.dtype) for a in args],
            pltpu.VMEM((tgt, ctrs), F32),
            pltpu.VMEM((128, npts), BF16),
            pltpu.VMEM((ctrs, 128), BF16),
            pltpu.VMEM((tgt, ctrs), BF16),
            *[pltpu.VMEM((ctrs, npts // PCH), BF16)] * PCH,
            pltpu.VMEM((GROUPS, PCH, tgt, npts // PCH), BF16),
            pltpu.VMEM((EARLY, tgt, ctrs // MCH), F32),
            pltpu.VMEM((MCH, PLANE, *share), F32),
            pltpu.VMEM((MCH, PLANE, *share), F32),
            pltpu.VMEM((MCH, DEPTH // STRIDE, *share), F32),
            pltpu.VMEM((MCH, STRIDE, *share), F32),
            pltpu.VMEM((DEPTH, *share), F32),
            pltpu.VMEM((MCH, PLANE, *share), F32),
            pltpu.VMEM((GROUPS, 1, LANES), F32),
            pltpu.VMEM((PLANE, 1, LANES), F32),
            dma((5,)),
            dma((MCH,)),
            dma((PCH, GROUPS)), dma((PCH, GROUPS)),
            dma((MCH, PLANE)), dma((MCH, PLANE)),
            dma((MCH, DEPTH // STRIDE)), dma((MCH, DEPTH // STRIDE)),
            dma((MCH, 2)), dma((MCH, 2)),
            dma((DEPTH,)), dma((DEPTH,)),
            dma((MCH, PLANE)), dma((MCH, PLANE)),
            dma((GROUPS,)), dma((GROUPS,)),
            dma((PLANE,)), dma((PLANE,)),
        ],
        compiler_params=pltpu.CompilerParams(
            collective_id=0, has_side_effects=True, vmem_limit_bytes=56 << 20
        ),
        name="cg_step",
    )(*args)
    return pl.pallas_call(
        update,
        out_shape=(whole,) * 3,
        grid=(UCH,),
        in_specs=[
            pl.BlockSpec((2, *share), lambda k: (0, 0, 0)),
            *[pl.BlockSpec((tgt, ctrs // UCH), lambda k: (0, k))] * 4,
            pl.BlockSpec((1, ctrs // UCH), lambda k: (0, k)),
        ],
        out_specs=(pl.BlockSpec((tgt, ctrs // UCH), lambda k: (0, k)),) * 3,
        compiler_params=pltpu.CompilerParams(vmem_limit_bytes=60 << 20),
        name="update",
    )(scal, image, coef, resid, direction, prec)


def solution(mesh):
    return jax.shard_map(
        shards,
        mesh=mesh,
        in_specs=(P(None, "pts"), *[P(None, "ctr")] * 4, P("ctr")),
        out_specs=(P(None, "ctr"),) * 3,
        check_vma=False,
    )
```

```python
import functools
import math

import jax
import jax.numpy as jnp
from jax import lax
from jax.experimental import pallas as pl
from jax.experimental.pallas import tpu as pltpu
from jax.sharding import PartitionSpec as P

MESH = pl.DeviceIdType.MESH
F32 = jnp.float32
BF16 = jnp.bfloat16
LOG2E = math.log2(math.e)

GROUPS = 4
PLANE = 16
DEPTH = 12
STRIDE = 3
PCH = 4
MCH = 4
EARLY = 2
UCH = 2
LANES = 128
EIGHTHS = (3, 2, 2, 1)
CROWS = 2048
IN_PLANE = (4, 12, 3, 5, 11, 13, 2, 6, 10, 14, 1, 7, 9, 15, 8)
ALONG_Z = (6, 5, 7, 4, 8, 3, 9, 2, 10, 1, 11)


def three_terms(v):
    hi = v.astype(BF16)
    rest = v - hi.astype(F32)
    mid = rest.astype(BF16)
    lo = (rest - mid.astype(F32)).astype(BF16)
    return hi, mid, lo


def tail_rows(width, first, second):
    row = lax.broadcasted_iota(jnp.int32, (32, width), 0)
    out = jnp.zeros((32, width), F32)
    for k, v in enumerate((*first, *second)):
        out = jnp.where(row == k, v if isinstance(v, float) else v.astype(F32), out)
    return out.astype(BF16)


def kernel(
    pts_hbm, cen_hbm, dir_hbm, res_hbm, prec_hbm, q_hbm, scal_ref,
    pts_ref, cen_ref, dir_ref, res_ref, prec_ref, q_ref,
    xa, ca, dirb, kern0, kern1, kern2, kern3, fit0, fit1, fit2, fit3, early, col, rsb, z1b, z2b, zb, agb, scb, spb,
    in_s, out_s, fit_s, fit_r, rs_s, rs_r, z1_s, z1_r, z2_s, z2_r, z_s, z_r, ag_s, ag_r, sc_s, sc_r, sp_s, sp_r,
):
    npts = pts_ref.shape[1]
    tgt, ctrs = dir_ref.shape
    width = [npts // 8 * k for k in EIGHTHS]
    begin = [sum(width[:k]) for k in range(PCH)]
    mch = ctrs // MCH
    kerns = (kern0, kern1, kern2, kern3)
    fits = (fit0, fit1, fit2, fit3)
    pts = lax.axis_index("pts")
    ctr = lax.axis_index("ctr")
    z = pts // PLANE
    mine = pts % PLANE
    third, step = z // STRIDE, z % STRIDE

    loads = [
        pltpu.make_async_copy(src, dst, in_s.at[k])
        for k, (src, dst) in enumerate(
            [(pts_hbm, pts_ref), (cen_hbm, cen_ref), (dir_hbm, dir_ref), (res_hbm, res_ref), (prec_hbm, prec_ref)]
        )
    ]
    for load in loads:
        load.start()

    def ctr_peer(d):
        return {"ctr": (ctr + d) % GROUPS}

    def plane_peer(d):
        return {"pts": z * PLANE + (mine + d) % PLANE}

    def z_peer(d):
        return {"pts": (z + d) % DEPTH * PLANE + mine}

    barrier = pltpu.get_barrier_semaphore()
    peers = [ctr_peer(d) for d in range(1, GROUPS)]
    peers += [plane_peer(d) for d in range(1, PLANE)]
    peers += [z_peer(d) for d in ALONG_Z]
    for peer in peers:
        pl.semaphore_signal(barrier, inc=1, device_id=peer, device_id_type=MESH)

    def send(src, dst, s, r, peer):
        return pltpu.make_async_remote_copy(
            src_ref=src, dst_ref=dst, send_sem=s, recv_sem=r, device_id=peer, device_id_type=MESH
        )

    loads[0].wait()
    x32 = pts_ref[...].astype(F32)
    hi, mid, lo = three_terms(x32 * (0.25 * LOG2E))
    xa[0:32, :] = hi
    xa[32:64, :] = mid
    xa[64:96, :] = lo
    xsq = jnp.sum(x32 * x32, axis=0, keepdims=True) * (-0.125 * LOG2E)
    xa[96:128, :] = tail_rows(npts, (1.0, 1.0, 1.0), three_terms(xsq))
    loads[1].wait()
    loads[2].wait()

    def centre_block(k, rows):
        at = slice(k * rows, (k + 1) * rows)
        c = cen_ref[:, at]
        c32 = c.astype(F32)
        csq = jnp.sum(c32 * c32, axis=0, keepdims=True) * (-0.125 * LOG2E)
        tail = tail_rows(rows, three_terms(csq), (1.0, 1.0, 1.0))
        block = jnp.concatenate([c, c, c, tail], axis=0).T
        ca[at, :] = block
        dirb[:, at] = dir_ref[:, at].astype(BF16)
        s = jnp.dot(block, xa[:, : width[0]], preferred_element_type=F32)
        kerns[0][at, :] = jnp.exp2(s).astype(BF16)

    def fit_copy(i, d):
        return send(
            fits[i].at[ctr], fits[i].at[ctr], fit_s.at[i, d], fit_r.at[i, d], ctr_peer(d)
        )

    for i in range(PCH + 1):
        if i == 0:
            for k in range(ctrs // CROWS):
                centre_block(k, CROWS)
        elif i < PCH:
            s = jnp.dot(ca[...], xa[:, begin[i] : begin[i] + width[i]], preferred_element_type=F32)
            kerns[i][...] = jnp.exp2(s).astype(BF16)
        if i > 0:
            part = jnp.dot(dirb[...], kerns[i - 1][...], preferred_element_type=F32)
        if i == 1:
            pl.semaphore_wait(barrier, len(peers))
        if i > 0:
            fits[i - 1][ctr] = part.astype(BF16)
            for d in range(1, GROUPS):
                fit_copy(i - 1, d).start()

    def fitted(i):
        for d in range(1, GROUPS):
            fit_copy(i, d).wait()
        total = fits[i][0].astype(F32)
        for g in range(1, GROUPS):
            total = total + fits[i][g].astype(F32)
        return total.astype(BF16)

    def rs_copy(c, d):
        return send(
            col.at[c, (mine + d) % PLANE], rsb.at[c, mine], rs_s.at[c, d], rs_r.at[c, d], plane_peer(d)
        )

    def z1_copy(c, d):
        return send(
            z1b.at[c, third], z1b.at[c, third], z1_s.at[c, d], z1_r.at[c, d], z_peer(d * STRIDE)
        )

    def z2_copy(c, d):
        return send(
            z2b.at[c, step], z2b.at[c, step], z2_s.at[c, d], z2_r.at[c, d], z_peer((1, DEPTH - 1)[d])
        )

    def z_copy(d):
        return send(zb.at[z], zb.at[z], z_s.at[d], z_r.at[d], z_peer(d))

    def ag_copy(c, d):
        return send(
            agb.at[c, mine], agb.at[c, mine], ag_s.at[c, d], ag_r.at[c, d], plane_peer(d)
        )

    def col_part(c, i, fit):
        return lax.dot_general(
            fit, kerns[i][c * mch : (c + 1) * mch, :], (((1,), (1,)), ((), ())), preferred_element_type=F32
        )

    def summed(ref, c, count):
        total = ref[c, 0]
        for k in range(1, count):
            total = total + ref[c, k]
        return total

    def to_rs(c, part):
        for j in range(PLANE):
            col[c, j] = part[:, j * LANES : (j + 1) * LANES]
        for d in IN_PLANE:
            rs_copy(c, d).start()
        rsb[c, mine] = col[c, mine]

    def to_z1(c):
        for d in range(1, PLANE):
            rs_copy(c, d).wait()
        if c == MCH - 1:
            zb[z] = summed(rsb, c, PLANE)
            for d in ALONG_Z:
                z_copy(d).start()
            return
        z1b[c, third] = summed(rsb, c, PLANE)
        for d in (2, 1, 3):
            z1_copy(c, d).start()

    def to_z2(c):
        for d in range(1, DEPTH // STRIDE):
            z1_copy(c, d).wait()
        z2b[c, step] = summed(z1b, c, DEPTH // STRIDE)
        for d in range(2):
            z2_copy(c, d).start()

    scale = 2048.0 / (npts * DEPTH * PLANE)

    def start_ag(c):
        for d in IN_PLANE:
            ag_copy(c, d).start()

    def to_ag(c, sums):
        if c == MCH - 1:
            for d in ALONG_Z:
                z_copy(d).wait()
            share = zb[0]
            for k in range(1, DEPTH):
                share = share + zb[k]
        else:
            for d in range(2):
                z2_copy(c, d).wait()
            share = summed(z2b, c, STRIDE)
        agb[c, mine] = share
        if c < MCH - 1:
            start_ag(c)
        at = pl.ds(pl.multiple_of(c * mch + mine * LANES, LANES), LANES)
        dirv, resv, prec = dir_ref[:, at], res_ref[:, at], prec_ref[:, at]
        image = share * scale + 0.5 * dirv
        pr = prec * resv
        new = (pr * resv, pr * image, prec * image * image, dirv * image)
        return [a + b for a, b in zip(sums, new)]

    fit = [fitted(i) for i in range(PCH - 1)]
    for c in range(EARLY):
        early[c] = sum((col_part(c, i, fit[i]) for i in range(1, PCH - 1)), col_part(c, 0, fit[0]))
    fit.append(fitted(PCH - 1))
    for c in range(EARLY):
        to_rs(c, early[c] + col_part(c, PCH - 1, fit[-1]))
    for c in range(EARLY, MCH):
        to_rs(c, sum((col_part(c, i, fit[i]) for i in range(1, PCH)), col_part(c, 0, fit[0])))
        if c == MCH - 2:
            to_z1(0)
    loads[3].wait()
    loads[4].wait()
    sums = [jnp.zeros((tgt, LANES), F32)] * 4
    to_z1(1)
    to_z2(0)
    to_z1(2)
    to_z2(1)
    sums = to_ag(0, sums)
    to_z1(3)
    to_z2(2)
    sums = to_ag(1, sums)
    sums = to_ag(2, sums)
    sums = to_ag(3, sums)

    lane = lax.broadcasted_iota(jnp.int32, (tgt, LANES), 1)
    spot = lane - lax.broadcasted_iota(jnp.int32, (tgt, LANES), 0)
    packed = jnp.zeros((tgt, LANES), F32)
    for k, v in enumerate(sums):
        packed = jnp.where(spot == k * tgt, jnp.sum(v, axis=1, keepdims=True), packed)
    spb[mine] = jnp.sum(packed, axis=0, keepdims=True)

    def sp_copy(d):
        return send(spb.at[mine], spb.at[mine], sp_s.at[d], sp_r.at[d], plane_peer(d))

    def sc_copy(d):
        return send(scb.at[ctr], scb.at[ctr], sc_s.at[d], sc_r.at[d], ctr_peer(d))

    for d in IN_PLANE:
        sp_copy(d).start()
    start_ag(MCH - 1)
    for d in range(1, PLANE):
        sp_copy(d).wait()
    total = spb[0]
    for k in range(1, PLANE):
        total = total + spb[k]
    scb[ctr] = total
    for d in range(1, GROUPS):
        sc_copy(d).start()

    def out_copy(c):
        at = pl.ds(pl.multiple_of(c * mch, mch), mch)
        return pltpu.make_async_copy(q_ref.at[:, at], q_hbm.at[:, at], out_s.at[c])

    def finish(c, carry):
        for d in range(1, PLANE):
            ag_copy(c, d).wait()
        for k in range(PLANE):
            at = pl.ds(pl.multiple_of(c * mch + k * LANES, LANES), LANES)
            q_ref[:, at] = agb[c, k] * scale + 0.5 * dir_ref[:, at]
        out_copy(c).start()
        return carry

    lax.fori_loop(0, MCH, finish, 0)
    for d in range(1, GROUPS):
        sc_copy(d).wait()
    total = scb[0] + scb[1] + scb[2] + scb[3]
    rr, rq, qq, dq = [
        jnp.sum(jnp.where(spot == k * tgt, total, 0.0), axis=1, keepdims=True) for k in range(4)
    ]
    alpha = rr / dq
    rz_new = rr - 2.0 * alpha * rq + alpha * alpha * qq
    scal_ref[0] = jnp.broadcast_to(alpha, (tgt, LANES))
    scal_ref[1] = jnp.broadcast_to(rz_new / rr, (tgt, LANES))
    for c in range(MCH):
        out_copy(c).wait()


def update(scal_ref, q_ref, coef_ref, res_ref, dir_ref, prec_ref, coef_out, res_out, dir_out):
    alpha, beta = scal_ref[0][:, :1], scal_ref[1][:, :1]
    dirv = dir_ref[...]
    res = res_ref[...] - alpha * q_ref[...]
    coef_out[...] = coef_ref[...] + alpha * dirv
    res_out[...] = res
    dir_out[...] = prec_ref[...] * res + beta * dirv


def shards(points, centres, coef, resid, direction, precond):
    tgt, ctrs = direction.shape
    npts = points.shape[1]
    prec = precond[None, :]
    vm = pl.BlockSpec(memory_space=pltpu.VMEM)
    dma = pltpu.SemaphoreType.DMA
    share = (tgt, LANES)
    whole = jax.ShapeDtypeStruct((tgt, ctrs), F32)
    args = (points, centres, direction, resid, prec)
    image, scal = pl.pallas_call(
        kernel,
        out_shape=(whole, jax.ShapeDtypeStruct((2, *share), F32)),
        in_specs=[pl.BlockSpec(memory_space=pl.ANY)] * 5,
        out_specs=(pl.BlockSpec(memory_space=pl.ANY), vm),
        scratch_shapes=[
            *[pltpu.VMEM(a.shape, a.dtype) for a in args],
            pltpu.VMEM((tgt, ctrs), F32),
            pltpu.VMEM((128, npts), BF16),
            pltpu.VMEM((ctrs, 128), BF16),
            pltpu.VMEM((tgt, ctrs), BF16),
            *[pltpu.VMEM((ctrs, npts // 8 * k), BF16) for k in EIGHTHS],
            *[pltpu.VMEM((GROUPS, tgt, npts // 8 * k), BF16) for k in EIGHTHS],
            pltpu.VMEM((EARLY, tgt, ctrs // MCH), F32),
            pltpu.VMEM((MCH, PLANE, *share), F32),
            pltpu.VMEM((MCH, PLANE, *share), F32),
            pltpu.VMEM((MCH, DEPTH // STRIDE, *share), F32),
            pltpu.VMEM((MCH, STRIDE, *share), F32),
            pltpu.VMEM((DEPTH, *share), F32),
            pltpu.VMEM((MCH, PLANE, *share), F32),
            pltpu.VMEM((GROUPS, 1, LANES), F32),
            pltpu.VMEM((PLANE, 1, LANES), F32),
            dma((5,)),
            dma((MCH,)),
            dma((PCH, GROUPS)), dma((PCH, GROUPS)),
            dma((MCH, PLANE)), dma((MCH, PLANE)),
            dma((MCH, DEPTH // STRIDE)), dma((MCH, DEPTH // STRIDE)),
            dma((MCH, 2)), dma((MCH, 2)),
            dma((DEPTH,)), dma((DEPTH,)),
            dma((MCH, PLANE)), dma((MCH, PLANE)),
            dma((GROUPS,)), dma((GROUPS,)),
            dma((PLANE,)), dma((PLANE,)),
        ],
        compiler_params=pltpu.CompilerParams(
            collective_id=0, has_side_effects=True, vmem_limit_bytes=56 << 20
        ),
        name="cg_step",
    )(*args)
    return pl.pallas_call(
        update,
        out_shape=(whole,) * 3,
        grid=(UCH,),
        in_specs=[
            pl.BlockSpec((2, *share), lambda k: (0, 0, 0)),
            *[pl.BlockSpec((tgt, ctrs // UCH), lambda k: (0, k))] * 4,
            pl.BlockSpec((1, ctrs // UCH), lambda k: (0, k)),
        ],
        out_specs=(pl.BlockSpec((tgt, ctrs // UCH), lambda k: (0, k)),) * 3,
        compiler_params=pltpu.CompilerParams(vmem_limit_bytes=60 << 20),
        name="update",
    )(scal, image, coef, resid, direction, prec)


def solution(mesh):
    return jax.shard_map(
        shards,
        mesh=mesh,
        in_specs=(P(None, "pts"), *[P(None, "ctr")] * 4, P("ctr")),
        out_specs=(P(None, "ctr"),) * 3,
        check_vma=False,
    )
```
